256 devices in a mesh: row: 32 (over x, z_hi, y), col: 8 (over z_lo, core).
Axes of the slice: x: 4, y: 4, z: 8 (z_hi: 2, z_lo: 4; z = z_hi * 4 + z_lo), core: 2. Of those that a mesh axis runs over, the one named last changes fastest.
Arguments:
- coupling: float32 [24576, 24576], P('row', 'col'), may hold values from -1 to 5, as said below
- vectors: float32 [24576, 256], P(('row', 'col')), may hold values from -6 to 6
Outputs:
- filtered: float32 [24576, 256], P(('row', 'col'))
- gram: float32 [256, 256], replicated
The draws below stay inside these ranges and needn't reach their ends.
Inputs may be any that keep to these rules, and one draw needn't show every extreme that they name: `coupling`: H, the operator with its column order restored, is symmetric.
All inputs are finite; a program needn't handle non-finite values.
Results may differ from the reference program's by a relative error of at most 0.0001.
Values sent between devices are 32-bit elements; how exact they have to be, the bound alone decides.
No kernel may reach another device: no remote copies, remote signals or barrier semaphores. Data moves between devices by JAX's collectives and lax.ppermute only.
A program may use at most 64 MiB of HBM per device.

```python
import math
import jax
import jax.numpy as jnp
from jax import lax

ORDER = 24576
VECS = 256
DEGREE = 6
N_ROW = 32
N_COL = 8


def draw_coupling(key, part):
    key_off, key_diag = jax.random.split(key, 2)
    raw_draw = jax.random.normal(key_off, (ORDER, ORDER), jnp.float32)
    spread = jnp.exp(jax.random.uniform(key_diag, (ORDER,), jnp.float32, math.log(0.7), math.log(1.4)))
    symmetric = (raw_draw + raw_draw.T) * (0.5 / math.sqrt(2.0 * ORDER))
    position = (jnp.arange(ORDER, dtype=jnp.float32) + 0.5) / ORDER
    diagonal = (0.3 + 2.7 * position) * spread
    on_diagonal = jnp.arange(ORDER)[:, None] == jnp.arange(ORDER)[None, :]
    operator_full = symmetric + jnp.where(on_diagonal, diagonal[None, :], 0.0)
    shard_rows = ORDER // (N_ROW * N_COL)
    return operator_full.reshape(ORDER, N_ROW, N_COL, shard_rows).transpose(0, 2, 1, 3).reshape(ORDER, ORDER)


def block_levels(own_key, dims, cuts, smallest, high):
    factor_of = 1.0
    for dim, parts in cuts:
        draws = jax.random.uniform(jax.random.fold_in(jax.random.fold_in(own_key, 6), dim), (parts,), jnp.float32, smallest / len(cuts), high / len(cuts))
        factor_of = factor_of * jnp.repeat(jnp.exp(draws), dims[dim] // parts).reshape((-1,) + (1,) * (len(dims) - 1 - dim))
    return factor_of


def scatter_about(rng, extent, scale, bound, pieces=(), kind=jnp.bfloat16):
    drawn = jax.random.normal(rng, extent, jnp.float32) * scale
    if len(pieces) > 0:
        drawn = block_levels(rng, extent, pieces, -0.22, 0.18) * drawn
    return jnp.clip(drawn, min=-bound, max=bound).astype(kind)


def setup_inputs(seed: int = 0) -> dict:
    streams_of = jax.random.split(jax.random.key(seed), 3)
    coupling = draw_coupling(jax.random.fold_in(streams_of[2], 71), 0)
    vectors = scatter_about(streams_of[1], (ORDER, VECS), 1.0, 6.0, ((0, 256),), jnp.float32)
    return {"coupling": coupling, "vectors": vectors}


filter_center = 2.75
filter_half = 1.75
filter_lower = 0.0


def reference(coupling, vectors):
    shard_rows = ORDER // (N_ROW * N_COL)

    def operate(current):
        stored = current.reshape(N_ROW, N_COL, shard_rows, VECS).transpose(1, 0, 2, 3).reshape(ORDER, VECS)
        product = jnp.dot(coupling, stored, precision=lax.Precision.HIGHEST, preferred_element_type=jnp.float32)
        return product - filter_center * current

    sigma_first = filter_half / (filter_lower - filter_center)
    previous = vectors
    current = (sigma_first / filter_half) * operate(vectors)
    sigma_now = sigma_first
    for degree_index in range(DEGREE - 1):
        sigma_new = 1.0 / (2.0 / sigma_first - sigma_now)
        following = (2.0 * sigma_new / filter_half) * operate(current) - (sigma_now * sigma_new) * previous
        previous = current
        current = following
        sigma_now = sigma_new
    gram = jnp.dot(current.T, current, precision=lax.Precision.HIGHEST, preferred_element_type=jnp.float32) / ORDER
    return current, gram
```

```python
import jax
import jax.numpy as jnp
from jax import lax
from jax.experimental import pallas as pl
from jax.experimental.pallas import tpu as pltpu
from jax.sharding import Mesh, PartitionSpec as P

ORDER = 24576
VECS = 256
DEGREE = 6
SH = 96
LOCAL = 768
COLS = 3072

filter_center = 2.75
filter_half = 1.75
filter_lower = 0.0


AX = ("x", "zh", "y", "zl", "core")
DIMS = (4, 2, 4, 4, 2)


def lin(x, zh, y, zl, core):
    return (((x * 2 + zh) * 4 + y) * 4 + zl) * 2 + core


def pairs(move):
    out = []
    for x in range(4):
        for zh in range(2):
            for y in range(4):
                for zl in range(4):
                    for core in range(2):
                        out.append((lin(x, zh, y, zl, core), lin(*move(x, zh, y, zl, core))))
    return out


SWAP_CORE = pairs(lambda x, zh, y, zl, core: (x, zh, y, zl, 1 - core))
SWAP_ZH = pairs(lambda x, zh, y, zl, core: (x, 1 - zh, y, zl, core))


def along_y(x, zh, y, zl, core, s):
    return (x, zh, (y + s) % 4, zl, core)


def along_x(x, zh, y, zl, core, s):
    return ((x + s) % 4, zh, y, zl, core)


FIRST = [pairs(lambda x, zh, y, zl, core, s=s: (along_x if core else along_y)(x, zh, y, zl, core, s)) for s in range(4)]
SECOND = [pairs(lambda x, zh, y, zl, core, s=s: (along_y if core else along_x)(x, zh, y, zl, core, s)) for s in range(4)]
ALONG_ZL = [pairs(lambda x, zh, y, zl, core, s=s: (x, zh, y, (zl + s) % 4, core)) for s in range(4)]


def send(value, moves):
    return lax.ppermute(value, AX, moves)


def split_kernel(h_ref, hi_ref, lo_ref):
    h = h_ref[...]
    hi = h.astype(jnp.bfloat16)
    hi_ref[...] = hi
    lo_ref[...] = (h - hi.astype(jnp.float32)).astype(jnp.bfloat16)


def split_operator(coupling):
    spec = pl.BlockSpec((96, COLS), lambda i: (i, 0))
    return pl.pallas_call(
        split_kernel,
        grid=(LOCAL // 96,),
        in_specs=[spec],
        out_specs=[spec, spec],
        out_shape=[jax.ShapeDtypeStruct((LOCAL, COLS), jnp.bfloat16)] * 2,
    )(coupling)


def product_kernel(place, g0, g1, g2, g3, h_hi, h_lo, keep, give, x_hi, x_lo):
    @pl.when(pl.program_id(0) == 0)
    def _():
        for t, g in enumerate((g0, g1, g2, g3)):
            for j in range(8):
                rows = g[j * SH : (j + 1) * SH, :]
                hi = rows.astype(jnp.bfloat16)
                lo = (rows - hi.astype(jnp.float32)).astype(jnp.bfloat16)
                at = pl.multiple_of(place[t * 8 + j], SH)
                x_hi[pl.ds(at, SH), :] = hi
                x_lo[pl.ds(at, SH), :] = lo

    acc = jnp.dot(h_hi[...], x_lo[...], preferred_element_type=jnp.float32)
    acc += jnp.dot(h_lo[...], x_hi[...], preferred_element_type=jnp.float32)
    acc += jnp.dot(h_hi[...], x_hi[...], preferred_element_type=jnp.float32)

    @pl.when(place[32] == 0)
    def _():
        keep[...] = acc[:SH]
        give[...] = acc[SH:]

    @pl.when(place[32] != 0)
    def _():
        keep[...] = acc[SH:]
        give[...] = acc[:SH]


def product(place, gathered, h_hi, h_lo):
    whole = pl.BlockSpec((LOCAL, VECS), lambda i, p: (0, 0))
    rows = pl.BlockSpec((2 * SH, COLS), lambda i, p: (i, 0))
    out = pl.BlockSpec((SH, VECS), lambda i, p: (i, 0))
    return pl.pallas_call(
        product_kernel,
        grid_spec=pltpu.PrefetchScalarGridSpec(
            num_scalar_prefetch=1,
            grid=(4,),
            in_specs=[whole] * 4 + [rows] * 2,
            out_specs=[out, out],
            scratch_shapes=[pltpu.VMEM((COLS, VECS), jnp.bfloat16)] * 2,
        ),
        out_shape=[jax.ShapeDtypeStruct((4 * SH, VECS), jnp.float32)] * 2,
        compiler_params=pltpu.CompilerParams(vmem_limit_bytes=32 << 20),
    )(place, *gathered, h_hi, h_lo)


def spread_kernel(place, keep, got, o0, o1, o2, o3):
    for s, o in enumerate((o0, o1, o2, o3)):
        at = pl.multiple_of(((place[33] + s) % 4) * SH, SH)
        o[...] = keep[pl.ds(at, SH), :] + got[pl.ds(at, SH), :]


def spread(place, keep, got):
    vmem = pl.BlockSpec(memory_space=pltpu.VMEM)
    return pl.pallas_call(
        spread_kernel,
        in_specs=[pl.BlockSpec(memory_space=pltpu.SMEM), vmem, vmem],
        out_specs=[vmem] * 4,
        out_shape=[jax.ShapeDtypeStruct((SH, VECS), jnp.float32)] * 4,
    )(place, keep, got)


def on_device(coupling, vectors):
    x, zh, y, zl, core = (lax.axis_index(a) for a in AX)
    j = jnp.arange(32, dtype=jnp.int32)
    t, s, zrel = j // 8, (j // 2) % 4, j % 2
    from_x = jnp.where(core == 0, x - t, x - s) % 4
    from_y = jnp.where(core == 0, y - s, y - t) % 4
    from_zh = (zh + zrel) % 2
    place = jnp.concatenate([((from_x * 2 + from_zh) * 4 + from_y) * SH, jnp.stack([core, zl])]).astype(jnp.int32)

    h_hi, h_lo = split_operator(coupling)

    def apply(current):
        plane = jnp.concatenate([current, send(current, SWAP_ZH)], axis=0)
        near = {s: send(plane, FIRST[s]) for s in (2, 1, 3)}
        first = jnp.concatenate([plane, near[1], near[2], near[3]], axis=0)
        far = {s: send(first, SECOND[s]) for s in (2, 1, 3)}
        keep, give = product(place, [first, far[1], far[2], far[3]], h_hi, h_lo)
        got = send(give, SWAP_CORE)
        parts = spread(place, keep, got)
        here = {s: send(parts[s], ALONG_ZL[s]) for s in (2, 1, 3)}
        return (parts[0] + here[1]) + (here[2] + here[3])

    sigma_first = filter_half / (filter_lower - filter_center)
    previous = vectors
    current = sigma_first / filter_half * (apply(vectors) - filter_center * vectors)
    sigma_now = sigma_first
    for _ in range(DEGREE - 1):
        sigma_new = 1.0 / (2.0 / sigma_first - sigma_now)
        following = 2.0 * sigma_new / filter_half * (apply(current) - filter_center * current) - sigma_now * sigma_new * previous
        previous = current
        current = following
        sigma_now = sigma_new

    local = jnp.dot(current.T, current, precision=lax.Precision.HIGHEST, preferred_element_type=jnp.float32)
    halves = local.reshape(2, 128, VECS)
    mine = lax.dynamic_index_in_dim(halves, core, 0, keepdims=False)
    other = lax.dynamic_index_in_dim(halves, 1 - core, 0, keepdims=False)
    half = mine + send(other, SWAP_CORE)
    piece = lax.all_to_all(half.reshape(16, 8, VECS), ("x", "y"), 0, 0).sum(axis=0)
    every = lax.all_to_all(jnp.broadcast_to(piece, (8, 8, VECS)), ("zh", "zl"), 0, 0).sum(axis=0) / ORDER
    half = lax.all_to_all(jnp.broadcast_to(every, (16, 8, VECS)), ("x", "y"), 0, 0).reshape(128, VECS)
    other = send(half, SWAP_CORE)
    gram = jnp.concatenate([jnp.where(core == 0, half, other), jnp.where(core == 0, other, half)], axis=0)
    return current, gram


def solution(mesh):
    fine = Mesh(mesh.devices.reshape(DIMS), AX)
    return jax.shard_map(
        on_device,
        mesh=fine,
        in_specs=(P(("x", "zh", "y"), ("zl", "core")), P(AX, None)),
        out_specs=(P(AX, None), P()),
        check_vma=False,
    )
```

```python
import functools

import jax
import jax.numpy as jnp
from jax import lax
from jax.experimental import pallas as pl
from jax.experimental.pallas import tpu as pltpu
from jax.sharding import Mesh, PartitionSpec as P

ORDER = 24576
VECS = 256
DEGREE = 6
SH = 96
LOCAL = 768
COLS = 3072

filter_center = 2.75
filter_half = 1.75
filter_lower = 0.0


AX = ("x", "zh", "y", "zl", "core")
DIMS = (4, 2, 4, 4, 2)


def lin(x, zh, y, zl, core):
    return (((x * 2 + zh) * 4 + y) * 4 + zl) * 2 + core


def pairs(move):
    out = []
    for x in range(4):
        for zh in range(2):
            for y in range(4):
                for zl in range(4):
                    for core in range(2):
                        out.append((lin(x, zh, y, zl, core), lin(*move(x, zh, y, zl, core))))
    return out


SWAP_CORE = pairs(lambda x, zh, y, zl, core: (x, zh, y, zl, 1 - core))
SWAP_ZH = pairs(lambda x, zh, y, zl, core: (x, 1 - zh, y, zl, core))


def along_y(x, zh, y, zl, core, s):
    return (x, zh, (y + s) % 4, zl, core)


def along_x(x, zh, y, zl, core, s):
    return ((x + s) % 4, zh, y, zl, core)


FIRST = [pairs(lambda x, zh, y, zl, core, s=s: (along_x if core else along_y)(x, zh, y, zl, core, s)) for s in range(4)]
SECOND = [pairs(lambda x, zh, y, zl, core, s=s: (along_y if core else along_x)(x, zh, y, zl, core, s)) for s in range(4)]
ALONG_ZL = [pairs(lambda x, zh, y, zl, core, s=s: (x, zh, y, (zl + s) % 4, core)) for s in range(4)]


def send(value, moves):
    return lax.ppermute(value, AX, moves)


HALF = 4 * SH


def split_kernel(place, h_ref, hi_ref, lo_ref):
    def write(h):
        hi = h.astype(jnp.bfloat16)
        hi_ref[...] = hi
        lo_ref[...] = (h - hi.astype(jnp.float32)).astype(jnp.bfloat16)

    @pl.when(place[0] == 0)
    def _():
        write(h_ref[...])

    @pl.when(place[0] != 0)
    def _():
        h = h_ref[...]
        order = [(x * 2 + zh) * 4 + y for y in range(4) for zh in range(2) for x in range(4)]
        write(jnp.concatenate([h[:, i * SH : (i + 1) * SH] for i in order], axis=1))


def split_operator(place, coupling):
    spec = pl.BlockSpec((96, COLS), lambda i, p: (i, 0))
    return pl.pallas_call(
        split_kernel,
        grid_spec=pltpu.PrefetchScalarGridSpec(
            num_scalar_prefetch=1, grid=(LOCAL // 96,), in_specs=[spec], out_specs=[spec, spec]
        ),
        out_shape=[jax.ShapeDtypeStruct((LOCAL, COLS), jnp.bfloat16)] * 2,
        compiler_params=pltpu.CompilerParams(vmem_limit_bytes=16 << 20),
    )(place, coupling)


def product_kernel(blocks, has_acc, last, *refs):
    place, h_hi, h_lo = refs[:3]
    parts = refs[3 : 3 + len(blocks)]
    refs = refs[3 + len(blocks) :]
    acc_in, refs = (refs[0], refs[1:]) if has_acc else (None, refs)
    outs, (x_hi, x_lo) = refs[:-2], refs[-2:]
    core, zl, zh, own_u, own_v = (place[i] for i in range(5))
    for b, part in enumerate(parts):
        for s in range(4):
            rows = part[s * SH : (s + 1) * SH, :]
            hi = rows.astype(jnp.bfloat16)
            lo = (rows - hi.astype(jnp.float32)).astype(jnp.bfloat16)
            at = pl.multiple_of(b * HALF + ((own_v - s + 4) % 4) * SH, SH)
            x_hi[pl.ds(at, SH), :] = hi
            x_lo[pl.ds(at, SH), :] = lo
    columns = [
        pl.multiple_of((((own_u - t + 4) % 4) * 2 + (zh + z) % 2) * HALF, HALF) for t, z in blocks
    ]

    def step(i, carry):
        at = pl.multiple_of(i * 2 * SH, 2 * SH)
        acc = acc_in[pl.ds(at, 2 * SH), :] if has_acc else None
        for b, column in enumerate(columns):
            hi = h_hi[pl.ds(at, 2 * SH), pl.ds(column, HALF)]
            lo = h_lo[pl.ds(at, 2 * SH), pl.ds(column, HALF)]
            xh, xl = x_hi[b * HALF : (b + 1) * HALF, :], x_lo[b * HALF : (b + 1) * HALF, :]
            for left, right in ((hi, xl), (lo, xh), (hi, xh)):
                term = jnp.dot(left, right, preferred_element_type=jnp.float32)
                acc = term if acc is None else acc + term
        if not last:
            outs[0][pl.ds(at, 2 * SH), :] = acc
            return carry
        keep, give = outs
        to = pl.multiple_of(((i - zl + 4) % 4) * SH, SH)

        @pl.when(core == 0)
        def _():
            keep[pl.ds(to, SH), :] = acc[:SH]
            give[pl.ds(to, SH), :] = acc[SH:]

        @pl.when(core != 0)
        def _():
            keep[pl.ds(to, SH), :] = acc[SH:]
            give[pl.ds(to, SH), :] = acc[:SH]

        return carry

    lax.fori_loop(0, 4, step, 0)


def product(place, h_hi, h_lo, parts, acc, last):
    vmem = pl.BlockSpec(memory_space=pltpu.VMEM)
    blocks = tuple(parts)
    args = [h_hi, h_lo, *parts.values()] + ([] if acc is None else [acc])
    shape = [(HALF, VECS)] * 2 if last else [(LOCAL, VECS)]
    return pl.pallas_call(
        functools.partial(product_kernel, blocks, acc is not None, last),
        in_specs=[pl.BlockSpec(memory_space=pltpu.SMEM)] + [vmem] * len(args),
        out_specs=[vmem] * len(shape),
        out_shape=[jax.ShapeDtypeStruct(a, jnp.float32) for a in shape],
        scratch_shapes=[pltpu.VMEM((len(blocks) * HALF, VECS), jnp.bfloat16)] * 2,
        compiler_params=pltpu.CompilerParams(vmem_limit_bytes=20 << 20),
    )(place, *args)


def on_device(coupling, vectors):
    x, zh, y, zl, core = (lax.axis_index(a) for a in AX)
    own_u, own_v = jnp.where(core == 0, x, y), jnp.where(core == 0, y, x)
    place = jnp.stack([core, zl, zh, own_u, own_v]).astype(jnp.int32)

    h_hi, h_lo = split_operator(place, coupling)

    def along_first(rows):
        near = {s: send(rows, FIRST[s]) for s in (2, 1, 3)}
        return jnp.concatenate([rows, near[1], near[2], near[3]], axis=0)

    def along_second(rows):
        return {s: send(rows, SECOND[s]) for s in (2, 1, 3)}

    def apply(current):
        partner = send(current, SWAP_ZH)
        a = along_first(current)
        far_a = along_second(a)
        b = along_first(partner)
        far_b = along_second(b)
        (acc,) = product(place, h_hi, h_lo, {(0, 0): a, (0, 1): b}, None, False)
        (acc,) = product(place, h_hi, h_lo, {(1, 0): far_a[1], (3, 0): far_a[3], (2, 0): far_a[2]}, acc, False)
        keep, give = product(place, h_hi, h_lo, {(1, 1): far_b[1], (3, 1): far_b[3], (2, 1): far_b[2]}, acc, True)
        total = keep + send(give, SWAP_CORE)
        here = {s: send(total[s * SH : (s + 1) * SH], ALONG_ZL[s]) for s in (2, 1, 3)}
        return (total[:SH] + here[1]) + (here[2] + here[3])

    sigma_first = filter_half / (filter_lower - filter_center)
    previous = vectors
    current = sigma_first / filter_half * (apply(vectors) - filter_center * vectors)
    sigma_now = sigma_first
    for _ in range(DEGREE - 1):
        sigma_new = 1.0 / (2.0 / sigma_first - sigma_now)
        following = 2.0 * sigma_new / filter_half * (apply(current) - filter_center * current) - sigma_now * sigma_new * previous
        previous = current
        current = following
        sigma_now = sigma_new

    local = jnp.dot(current.T, current, precision=lax.Precision.HIGHEST, preferred_element_type=jnp.float32)
    halves = local.reshape(2, 128, VECS)
    mine = lax.dynamic_index_in_dim(halves, core, 0, keepdims=False)
    other = lax.dynamic_index_in_dim(halves, 1 - core, 0, keepdims=False)
    half = mine + send(other, SWAP_CORE)
    piece = lax.all_to_all(half.reshape(16, 8, VECS), ("x", "y"), 0, 0).sum(axis=0)
    every = lax.all_to_all(jnp.broadcast_to(piece, (8, 8, VECS)), ("zh", "zl"), 0, 0).sum(axis=0) / ORDER
    half = lax.all_to_all(jnp.broadcast_to(every, (16, 8, VECS)), ("x", "y"), 0, 0).reshape(128, VECS)
    other = send(half, SWAP_CORE)
    gram = jnp.concatenate([jnp.where(core == 0, half, other), jnp.where(core == 0, other, half)], axis=0)
    return current, gram


def solution(mesh):
    fine = Mesh(mesh.devices.reshape(DIMS), AX)
    return jax.shard_map(
        on_device,
        mesh=fine,
        in_specs=(P(("x", "zh", "y"), ("zl", "core")), P(AX, None)),
        out_specs=(P(AX, None), P()),
        check_vma=False,
    )
```

```python
import functools

import jax
import jax.numpy as jnp
from jax import lax
from jax.experimental import pallas as pl
from jax.experimental.pallas import tpu as pltpu
from jax.sharding import Mesh, PartitionSpec as P


ORDER = 24576
VECS = 256
DEGREE = 6
SH = 96
LOCAL = 768
COLS = 3072

filter_center = 2.75
filter_half = 1.75
filter_lower = 0.0


AX = ("x", "zh", "y", "zl", "core")
DIMS = (4, 2, 4, 4, 2)


def lin(x, zh, y, zl, core):
    return (((x * 2 + zh) * 4 + y) * 4 + zl) * 2 + core


def pairs(move):
    out = []
    for x in range(4):
        for zh in range(2):
            for y in range(4):
                for zl in range(4):
                    for core in range(2):
                        out.append((lin(x, zh, y, zl, core), lin(*move(x, zh, y, zl, core))))
    return out


SWAP_CORE = pairs(lambda x, zh, y, zl, core: (x, zh, y, zl, 1 - core))
SWAP_ZH = pairs(lambda x, zh, y, zl, core: (x, 1 - zh, y, zl, core))


def along_y(x, zh, y, zl, core, s):
    return (x, zh, (y + s) % 4, zl, core)


def along_x(x, zh, y, zl, core, s):
    return ((x + s) % 4, zh, y, zl, core)


FIRST = [pairs(lambda x, zh, y, zl, core, s=s: (along_x if core else along_y)(x, zh, y, zl, core, s)) for s in range(4)]
SECOND = [pairs(lambda x, zh, y, zl, core, s=s: (along_y if core else along_x)(x, zh, y, zl, core, s)) for s in range(4)]
ALONG_ZL = [pairs(lambda x, zh, y, zl, core, s=s: (x, zh, y, (zl + s) % 4, core)) for s in range(4)]


def send(value, moves):
    return lax.ppermute(value, AX, moves)


HALF = 4 * SH
BLOCKS = COLS // HALF


def split_kernel(place, h_ref, hi_ref, lo_ref):
    def write(order):
        h = h_ref[...]
        for block in range(BLOCKS):
            part = jnp.concatenate([h[:, i * SH : (i + 1) * SH] for i in order[4 * block : 4 * block + 4]], axis=1)
            hi = part.astype(jnp.bfloat16)
            hi_ref[block] = hi
            lo_ref[block] = (part - hi.astype(jnp.float32)).astype(jnp.bfloat16)

    @pl.when(place[0] == 0)
    def _():
        write(list(range(32)))

    @pl.when(place[0] != 0)
    def _():
        write([(x * 2 + zh) * 4 + y for y in range(4) for zh in range(2) for x in range(4)])


def split_operator(place, coupling):
    out = pl.BlockSpec((BLOCKS, 96, HALF), lambda i, p: (0, i, 0))
    return pl.pallas_call(
        split_kernel,
        grid_spec=pltpu.PrefetchScalarGridSpec(
            num_scalar_prefetch=1,
            grid=(LOCAL // 96,),
            in_specs=[pl.BlockSpec((96, COLS), lambda i, p: (i, 0))],
            out_specs=[out, out],
        ),
        out_shape=[jax.ShapeDtypeStruct((BLOCKS, LOCAL, HALF), jnp.bfloat16)] * 2,
        compiler_params=pltpu.CompilerParams(vmem_limit_bytes=16 << 20),
    )(place, coupling)


def product_kernel(blocks, fetch, ready, has_acc, last, *refs):
    place, h_hi, h_lo = refs[:3]
    n = sum(count for _, _, count in blocks)
    parts, refs = refs[3 : 3 + n], refs[3 + n :]
    acc_in, refs = (refs[0], refs[1:]) if has_acc else (None, refs)
    outs, refs = refs[:2] if last else refs[:1], refs[2 if last else 1 :]
    ahead, refs = (refs[:2], refs[2:]) if fetch else (None, refs)
    x_hi, x_lo = refs[:2]
    core, zl, zh, own_u, own_v = (place[i] for i in range(5))

    def block_of(t, z):
        return ((own_u - t + 4) % 4) * 2 + (zh + z) % 2

    copies = []
    if ready:
        left_of = lambda b, at: (h_hi[pl.ds(at, 2 * SH), :], h_lo[pl.ds(at, 2 * SH), :])
    else:
        b_hi, b_lo, sems = refs[2:5]
        for b, (t, z, _) in enumerate(blocks):
            for k, (h, to) in enumerate(((h_hi, b_hi), (h_lo, b_lo))):
                copies.append(pltpu.make_async_copy(h.at[block_of(t, z)], to.at[b], sems.at[b, k]))
        left_of = lambda b, at: (b_hi[b, pl.ds(at, 2 * SH), :], b_lo[b, pl.ds(at, 2 * SH), :])
    if fetch:
        for k, (h, to) in enumerate(((h_hi, ahead[0]), (h_lo, ahead[1]))):
            copies.append(pltpu.make_async_copy(h.at[block_of(*fetch)], to, sems.at[len(blocks), k]))
    for copy in copies:
        copy.start()

    pieces = iter(parts)
    for b, (_, _, count) in enumerate(blocks):
        for s in range(4):
            if s % (4 // count) == 0:
                part = next(pieces)
            first = s % (4 // count) * SH
            rows = part[first : first + SH, :]
            hi = rows.astype(jnp.bfloat16)
            lo = (rows - hi.astype(jnp.float32)).astype(jnp.bfloat16)
            at = pl.multiple_of(b * HALF + ((own_v - s + 4) % 4) * SH, SH)
            x_hi[pl.ds(at, SH), :] = hi
            x_lo[pl.ds(at, SH), :] = lo

    for b in range(len(blocks)):
        if not ready:
            copies[2 * b].wait()
            copies[2 * b + 1].wait()
        xh, xl = x_hi[b * HALF : (b + 1) * HALF, :], x_lo[b * HALF : (b + 1) * HALF, :]

        def step(i, carry, b=b, xh=xh, xl=xl):
            at = pl.multiple_of(i * 2 * SH, 2 * SH)
            hi, lo = left_of(b, at)
            acc = jnp.dot(hi, xl, preferred_element_type=jnp.float32)
            acc += jnp.dot(lo, xh, preferred_element_type=jnp.float32)
            acc += jnp.dot(hi, xh, preferred_element_type=jnp.float32)
            if b:
                acc += outs[0][pl.ds(at, 2 * SH), :]
            elif has_acc:
                acc += acc_in[pl.ds(at, 2 * SH), :]
            if not last:
                outs[0][pl.ds(at, 2 * SH), :] = acc
                return carry
            keep, give = outs
            to = pl.multiple_of(((i - zl + 4) % 4) * SH, SH)

            @pl.when(core == 0)
            def _():
                keep[pl.ds(to, SH), :] = acc[:SH]
                give[pl.ds(to, SH), :] = acc[SH:]

            @pl.when(core != 0)
            def _():
                keep[pl.ds(to, SH), :] = acc[SH:]
                give[pl.ds(to, SH), :] = acc[:SH]

            return carry

        lax.fori_loop(0, 4, step, 0)
    for copy in copies[2 * len(blocks) :] if fetch else []:
        copy.wait()


def product(place, h_hi, h_lo, blocks, acc, fetch=None, last=False):
    vmem = pl.BlockSpec(memory_space=pltpu.VMEM)
    given = [a for _, _, arrays in blocks for a in arrays] + ([] if acc is None else [acc])
    out = [jax.ShapeDtypeStruct((HALF, VECS), jnp.float32)] * 2 if last else [jax.ShapeDtypeStruct((LOCAL, VECS), jnp.float32)]
    if fetch:
        out = out + [jax.ShapeDtypeStruct((LOCAL, HALF), jnp.bfloat16)] * 2
    scratch = [pltpu.VMEM((len(blocks) * HALF, VECS), jnp.bfloat16)] * 2
    if not last:
        scratch += [pltpu.VMEM((len(blocks), LOCAL, HALF), jnp.bfloat16)] * 2 + [pltpu.SemaphoreType.DMA((len(blocks) + 1, 2))]
    kernel = functools.partial(
        product_kernel, tuple((t, z, len(arrays)) for t, z, arrays in blocks), fetch, last, acc is not None, last
    )
    return pl.pallas_call(
        kernel,
        in_specs=[pl.BlockSpec(memory_space=pltpu.SMEM)]
        + [vmem if last else pl.BlockSpec(memory_space=pl.ANY)] * 2
        + [vmem] * len(given),
        out_specs=[vmem] * len(out),
        out_shape=out,
        scratch_shapes=scratch,
        compiler_params=pltpu.CompilerParams(vmem_limit_bytes=20 << 20),
    )(place, h_hi, h_lo, *given)


def on_device(coupling, vectors):
    x, zh, y, zl, core = (lax.axis_index(a) for a in AX)
    own_u, own_v = jnp.where(core == 0, x, y), jnp.where(core == 0, y, x)
    place = jnp.stack([core, zl, zh, own_u, own_v]).astype(jnp.int32)

    h_hi, h_lo = split_operator(place, coupling)

    def along_first(rows):
        near = {s: send(rows, FIRST[s]) for s in (2, 1, 3)}
        return jnp.concatenate([rows, near[1], near[2], near[3]], axis=0)

    def beside(rows):
        return send(rows, SECOND[1]), send(rows, SECOND[3])

    def opposite(low, high):
        return send(low[: 2 * SH], SECOND[1]), send(high[2 * SH :], SECOND[3])

    def apply(current):
        partner = send(current, SWAP_ZH)
        a = along_first(current)
        a1, a3 = beside(a)
        b = along_first(partner)
        b1, b3 = beside(b)
        a2 = opposite(a1, a3)
        (acc,) = product(place, h_hi, h_lo, [(0, 0, [a]), (0, 1, [b]), (1, 0, [a1]), (3, 0, [a3])], None)
        acc, b1, b3 = lax.optimization_barrier((acc, b1, b3))
        b2 = opposite(b1, b3)
        acc, f_hi, f_lo = product(place, h_hi, h_lo, [(1, 1, [b1]), (3, 1, [b3]), (2, 0, a2)], acc, fetch=(2, 1))
        keep, give = product(place, f_hi, f_lo, [(2, 1, b2)], acc, last=True)
        total = keep + send(give, SWAP_CORE)
        here = {s: send(total[s * SH : (s + 1) * SH], ALONG_ZL[s]) for s in (2, 1, 3)}
        return (total[:SH] + here[1]) + (here[2] + here[3])

    sigma_first = filter_half / (filter_lower - filter_center)
    gains, losses = [sigma_first / filter_half], [0.0]
    sigma_now = sigma_first
    for _ in range(DEGREE - 1):
        sigma_new = 1.0 / (2.0 / sigma_first - sigma_now)
        gains.append(2.0 * sigma_new / filter_half)
        losses.append(sigma_now * sigma_new)
        sigma_now = sigma_new
    gains, losses = jnp.array(gains, jnp.float32), jnp.array(losses, jnp.float32)

    def step(i, carry):
        previous, current = carry
        applied = apply(current)
        following = gains[i] * (applied - filter_center * current) - losses[i] * previous
        return current, following

    _, current = lax.fori_loop(0, DEGREE, step, (vectors, vectors))

    local = jnp.dot(current.T, current, precision=lax.Precision.HIGHEST, preferred_element_type=jnp.float32)
    halves = local.reshape(2, 128, VECS)
    mine = lax.dynamic_index_in_dim(halves, core, 0, keepdims=False)
    other = lax.dynamic_index_in_dim(halves, 1 - core, 0, keepdims=False)
    half = mine + send(other, SWAP_CORE)
    piece = lax.all_to_all(half.reshape(16, 8, VECS), ("x", "y"), 0, 0).sum(axis=0)
    every = lax.all_to_all(jnp.broadcast_to(piece, (8, 8, VECS)), ("zh", "zl"), 0, 0).sum(axis=0) / ORDER
    half = lax.all_to_all(jnp.broadcast_to(every, (16, 8, VECS)), ("x", "y"), 0, 0).reshape(128, VECS)
    other = send(half, SWAP_CORE)
    gram = jnp.concatenate([jnp.where(core == 0, half, other), jnp.where(core == 0, other, half)], axis=0)
    return current, gram


def solution(mesh):
    fine = Mesh(mesh.devices.reshape(DIMS), AX)
    return jax.shard_map(
        on_device,
        mesh=fine,
        in_specs=(P(("x", "zh", "y"), ("zl", "core")), P(AX, None)),
        out_specs=(P(AX, None), P()),
        check_vma=False,
    )
```

```python
import functools

import jax
import jax.numpy as jnp
from jax import lax
from jax.experimental import pallas as pl
from jax.experimental.pallas import tpu as pltpu
from jax.sharding import Mesh, PartitionSpec as P


ORDER = 24576
VECS = 256
DEGREE = 6
SH = 96
LOCAL = 768
COLS = 3072

filter_center = 2.75
filter_half = 1.75
filter_lower = 0.0


AX = ("x", "zh", "y", "zl", "core")
DIMS = (4, 2, 4, 4, 2)


def lin(x, zh, y, zl, core):
    return (((x * 2 + zh) * 4 + y) * 4 + zl) * 2 + core


def pairs(move):
    out = []
    for x in range(4):
        for zh in range(2):
            for y in range(4):
                for zl in range(4):
                    for core in range(2):
                        out.append((lin(x, zh, y, zl, core), lin(*move(x, zh, y, zl, core))))
    return out


SWAP_CORE = pairs(lambda x, zh, y, zl, core: (x, zh, y, zl, 1 - core))
SWAP_ZH = pairs(lambda x, zh, y, zl, core: (x, 1 - zh, y, zl, core))


def along_y(x, zh, y, zl, core, s):
    return (x, zh, (y + s) % 4, zl, core)


def along_x(x, zh, y, zl, core, s):
    return ((x + s) % 4, zh, y, zl, core)


FIRST = [pairs(lambda x, zh, y, zl, core, s=s: (along_x if core else along_y)(x, zh, y, zl, core, s)) for s in range(4)]
SECOND = [pairs(lambda x, zh, y, zl, core, s=s: (along_y if core else along_x)(x, zh, y, zl, core, s)) for s in range(4)]
ALONG_ZL = [pairs(lambda x, zh, y, zl, core, s=s: (x, zh, y, (zl + s) % 4, core)) for s in range(4)]


def send(value, moves):
    return lax.ppermute(value, AX, moves)


HALF = 4 * SH
BLOCKS = COLS // HALF
DEEP = 3 * HALF


def split_kernel(place, h_ref, out_ref):
    def write(order):
        h = h_ref[...]
        for block in range(BLOCKS):
            part = jnp.concatenate([h[:, i * SH : (i + 1) * SH] for i in order[4 * block : 4 * block + 4]], axis=1)
            hi = part.astype(jnp.bfloat16)
            out_ref[block, :, :HALF] = hi
            out_ref[block, :, HALF : 2 * HALF] = (part - hi.astype(jnp.float32)).astype(jnp.bfloat16)
            out_ref[block, :, 2 * HALF :] = hi

    @pl.when(place[0] == 0)
    def _():
        write(list(range(32)))

    @pl.when(place[0] != 0)
    def _():
        write([(x * 2 + zh) * 4 + y for y in range(4) for zh in range(2) for x in range(4)])


def split_operator(place, coupling):
    return pl.pallas_call(
        split_kernel,
        grid_spec=pltpu.PrefetchScalarGridSpec(
            num_scalar_prefetch=1,
            grid=(LOCAL // 96,),
            in_specs=[pl.BlockSpec((96, COLS), lambda i, p: (i, 0))],
            out_specs=pl.BlockSpec((BLOCKS, 96, DEEP), lambda i, p: (0, i, 0)),
        ),
        out_shape=jax.ShapeDtypeStruct((BLOCKS, LOCAL, DEEP), jnp.bfloat16),
        compiler_params=pltpu.CompilerParams(vmem_limit_bytes=16 << 20),
    )(place, coupling)


def product_kernel(blocks, has_acc, last, *refs):
    place, operator = refs[:2]
    parts, refs = refs[2 : 2 + len(blocks)], refs[2 + len(blocks) :]
    acc_in, refs = (refs[0], refs[1:]) if has_acc else (None, refs)
    outs, rows_of = refs[:-1], refs[-1]
    core, zl, zh, own_u, own_v = (place[i] for i in range(5))
    for b, part in enumerate(parts):
        for s in range(4):
            rows = part[s * SH : (s + 1) * SH, :]
            hi = rows.astype(jnp.bfloat16)
            lo = (rows - hi.astype(jnp.float32)).astype(jnp.bfloat16)
            at = pl.multiple_of(((own_v - s + 4) % 4) * SH, SH)
            rows_of[b, pl.ds(at, SH), :] = lo
            rows_of[b, pl.ds(HALF + at, SH), :] = hi
            rows_of[b, pl.ds(2 * HALF + at, SH), :] = hi
    for half in range(2):
        m = slice(half * LOCAL // 2, (half + 1) * LOCAL // 2)
        acc = acc_in[m, :] if has_acc else None
        for b, (t, z) in enumerate(blocks):
            block = ((own_u - t + 4) % 4) * 2 + (zh + z) % 2
            term = jnp.dot(operator[block, m, :], rows_of[b], preferred_element_type=jnp.float32)
            acc = term if acc is None else acc + term
        if not last:
            outs[0][m, :] = acc
            continue
        keep, give = outs
        for pair in range(2):
            to = pl.multiple_of(((half * 2 + pair - zl + 4) % 4) * SH, SH)
            even, odd = acc[pair * 2 * SH : pair * 2 * SH + SH], acc[pair * 2 * SH + SH : (pair + 1) * 2 * SH]

            @pl.when(core == 0)
            def _():
                keep[pl.ds(to, SH), :] = even
                give[pl.ds(to, SH), :] = odd

            @pl.when(core != 0)
            def _():
                keep[pl.ds(to, SH), :] = odd
                give[pl.ds(to, SH), :] = even


def product(place, operator, parts, acc, last=False):
    vmem = pl.BlockSpec(memory_space=pltpu.VMEM)
    args = [operator, *parts.values()] + ([] if acc is None else [acc])
    shape = [(HALF, VECS)] * 2 if last else [(LOCAL, VECS)]
    out = pl.pallas_call(
        functools.partial(product_kernel, tuple(parts), acc is not None, last),
        in_specs=[pl.BlockSpec(memory_space=pltpu.SMEM)] + [vmem] * len(args),
        out_specs=[vmem] * len(shape),
        out_shape=[jax.ShapeDtypeStruct(a, jnp.float32) for a in shape],
        scratch_shapes=[pltpu.VMEM((len(parts), DEEP, VECS), jnp.bfloat16)],
        compiler_params=pltpu.CompilerParams(vmem_limit_bytes=20 << 20),
    )(place, *args)
    return out if last else out[0]


def on_device(coupling, vectors):
    x, zh, y, zl, core = (lax.axis_index(a) for a in AX)
    own_u, own_v = jnp.where(core == 0, x, y), jnp.where(core == 0, y, x)
    place = jnp.stack([core, zl, zh, own_u, own_v]).astype(jnp.int32)

    operator = split_operator(place, coupling)

    def along_first(rows):
        near = {s: send(rows, FIRST[s]) for s in (2, 1, 3)}
        return jnp.concatenate([rows, near[1], near[2], near[3]], axis=0)

    def along_second(rows):
        return {s: send(rows, SECOND[s]) for s in (2, 1, 3)}

    def apply(current):
        partner = send(current, SWAP_ZH)
        a = along_first(current)
        b = along_first(partner)
        far_a = along_second(a)
        far_b = along_second(b)
        acc = product(place, operator, {(0, 0): a, (0, 1): b}, None)
        acc = product(place, operator, {(t, 0): far_a[t] for t in (1, 3, 2)}, acc)
        acc = product(place, operator, {(t, 1): far_b[t] for t in (1, 3)}, acc)
        keep, give = product(place, operator, {(2, 1): far_b[2]}, acc, last=True)
        total = keep + send(give, SWAP_CORE)
        here = {s: send(total[s * SH : (s + 1) * SH], ALONG_ZL[s]) for s in (2, 1, 3)}
        return (total[:SH] + here[1]) + (here[2] + here[3])

    sigma_first = filter_half / (filter_lower - filter_center)
    gains, losses = [sigma_first / filter_half], [0.0]
    sigma_now = sigma_first
    for _ in range(DEGREE - 1):
        sigma_new = 1.0 / (2.0 / sigma_first - sigma_now)
        gains.append(2.0 * sigma_new / filter_half)
        losses.append(sigma_now * sigma_new)
        sigma_now = sigma_new

    previous, current = vectors, vectors
    for gain, loss in zip(gains, losses):
        applied = apply(current)
        following = gain * (applied - filter_center * current)
        if loss:
            following = following - loss * previous
        previous, current = current, following

    local = jnp.dot(current.T, current, precision=lax.Precision.HIGHEST, preferred_element_type=jnp.float32)
    halves = local.reshape(2, 128, VECS)
    mine = lax.dynamic_index_in_dim(halves, core, 0, keepdims=False)
    other = lax.dynamic_index_in_dim(halves, 1 - core, 0, keepdims=False)
    half = mine + send(other, SWAP_CORE)
    piece = lax.all_to_all(half.reshape(16, 8, VECS), ("x", "y"), 0, 0).sum(axis=0)
    every = lax.all_to_all(jnp.broadcast_to(piece, (8, 8, VECS)), ("zh", "zl"), 0, 0).sum(axis=0) / ORDER
    half = lax.all_to_all(jnp.broadcast_to(every, (16, 8, VECS)), ("x", "y"), 0, 0).reshape(128, VECS)
    other = send(half, SWAP_CORE)
    gram = jnp.concatenate([jnp.where(core == 0, half, other), jnp.where(core == 0, other, half)], axis=0)
    return current, gram


def solution(mesh):
    fine = Mesh(mesh.devices.reshape(DIMS), AX)
    return jax.shard_map(
        on_device,
        mesh=fine,
        in_specs=(P(("x", "zh", "y"), ("zl", "core")), P(AX, None)),
        out_specs=(P(AX, None), P()),
        check_vma=False,
    )
```

```python
import functools

import jax
import jax.numpy as jnp
from jax import lax
from jax.experimental import pallas as pl
from jax.experimental.pallas import tpu as pltpu
from jax.sharding import Mesh, PartitionSpec as P


ORDER = 24576
VECS = 256
DEGREE = 6
SH = 96
LOCAL = 768
COLS = 3072

filter_center = 2.75
filter_half = 1.75
filter_lower = 0.0


AX = ("x", "zh", "y", "zl", "core")
DIMS = (4, 2, 4, 4, 2)


def lin(x, zh, y, zl, core):
    return (((x * 2 + zh) * 4 + y) * 4 + zl) * 2 + core


def pairs(move):
    out = []
    for x in range(4):
        for zh in range(2):
            for y in range(4):
                for zl in range(4):
                    for core in range(2):
                        out.append((lin(x, zh, y, zl, core), lin(*move(x, zh, y, zl, core))))
    return out


SWAP_CORE = pairs(lambda x, zh, y, zl, core: (x, zh, y, zl, 1 - core))
SWAP_ZH = pairs(lambda x, zh, y, zl, core: (x, 1 - zh, y, zl, core))


def along_y(x, zh, y, zl, core, s):
    return (x, zh, (y + s) % 4, zl, core)


def along_x(x, zh, y, zl, core, s):
    return ((x + s) % 4, zh, y, zl, core)


FIRST = [pairs(lambda x, zh, y, zl, core, s=s: (along_x if core else along_y)(x, zh, y, zl, core, s)) for s in range(4)]
SECOND = [pairs(lambda x, zh, y, zl, core, s=s: (along_y if core else along_x)(x, zh, y, zl, core, s)) for s in range(4)]
ALONG_ZL = [pairs(lambda x, zh, y, zl, core, s=s: (x, zh, y, (zl + s) % 4, core)) for s in range(4)]


def send(value, moves):
    return lax.ppermute(value, AX, moves)


HALF = 4 * SH
BLOCKS = COLS // HALF


def position():
    x, zh, y, zl, core = (lax.axis_index(a) for a in AX)
    return core, zl, zh, jnp.where(core == 0, x, y), jnp.where(core == 0, y, x)


def split_kernel(h_ref, out_ref):
    core = position()[0]

    def write(order):
        h = h_ref[...]
        for block in range(BLOCKS):
            part = jnp.concatenate([h[:, i * SH : (i + 1) * SH] for i in order[4 * block : 4 * block + 4]], axis=1)
            hi = part.astype(jnp.bfloat16)
            out_ref[block, :, :HALF] = hi
            out_ref[block, :, HALF:] = (part - hi.astype(jnp.float32)).astype(jnp.bfloat16)

    @pl.when(core == 0)
    def _():
        write(list(range(32)))

    @pl.when(core != 0)
    def _():
        write([(x * 2 + zh) * 4 + y for y in range(4) for zh in range(2) for x in range(4)])


def split_operator(coupling):
    return pl.pallas_call(
        split_kernel,
        grid=(LOCAL // 96,),
        in_specs=[pl.BlockSpec((96, COLS), lambda i: (i, 0))],
        out_specs=pl.BlockSpec((BLOCKS, 96, 2 * HALF), lambda i: (0, i, 0)),
        out_shape=jax.ShapeDtypeStruct((BLOCKS, LOCAL, 2 * HALF), jnp.bfloat16),
        compiler_params=pltpu.CompilerParams(vmem_limit_bytes=16 << 20),
    )(coupling)


def product_kernel(blocks, fetch, has_acc, last, *refs):
    operator, refs = refs[0], refs[1:]
    n = sum(count for _, _, count in blocks)
    parts, refs = refs[:n], refs[n:]
    acc_in, refs = (refs[0], refs[1:]) if has_acc else (None, refs)
    outs, refs = (refs[:2], refs[2:]) if last else (refs[:1], refs[1:])
    core, zl, zh, own_u, own_v = position()

    def block_of(t, z):
        return ((own_u - t + 4) % 4) * 2 + (zh + z) % 2

    copies = []
    if fetch:
        whole, refs = refs[0], refs[1:]
        sems = refs[1]
        for k in range(BLOCKS):
            block = block_of(k // 2, k % 2)
            copies.append(pltpu.make_async_copy(operator.at[block], whole.at[block], sems.at[k]))
            copies[-1].start()
        operator = whole
    rows_of = refs[0]

    pieces = iter(parts)
    for b, (_, _, count) in enumerate(blocks):
        for s in range(4):
            if s % (4 // count) == 0:
                part = next(pieces)
            first = s % (4 // count) * SH
            rows = part[first : first + SH, :]
            hi = rows.astype(jnp.bfloat16)
            lo = (rows - hi.astype(jnp.float32)).astype(jnp.bfloat16)
            at = pl.multiple_of(((own_v - s + 4) % 4) * SH, SH)
            rows_of[b, pl.ds(at, SH), :] = lo
            rows_of[b, pl.ds(HALF + at, SH), :] = hi
    for copy in copies[: len(blocks)]:
        copy.wait()
    for half in range(2):
        m = slice(half * LOCAL // 2, (half + 1) * LOCAL // 2)
        acc = acc_in[m, :] if has_acc else None
        for b, (t, z, _) in enumerate(blocks):
            block = block_of(t, z)
            term = jnp.dot(operator[block, m, :], rows_of[b], preferred_element_type=jnp.float32)
            term += jnp.dot(operator[block, m, :HALF], rows_of[b, HALF:, :], preferred_element_type=jnp.float32)
            acc = term if acc is None else acc + term
        if not last:
            outs[0][m, :] = acc
            continue
        keep, give = outs
        for pair in range(2):
            to = pl.multiple_of(((half * 2 + pair - zl + 4) % 4) * SH, SH)
            even, odd = acc[pair * 2 * SH : pair * 2 * SH + SH], acc[pair * 2 * SH + SH : (pair + 1) * 2 * SH]

            @pl.when(core == 0)
            def _():
                keep[pl.ds(to, SH), :] = even
                give[pl.ds(to, SH), :] = odd

            @pl.when(core != 0)
            def _():
                keep[pl.ds(to, SH), :] = odd
                give[pl.ds(to, SH), :] = even

    for copy in copies[len(blocks) :]:
        copy.wait()


def product(operator, blocks, acc, fetch=False, last=False):
    vmem = pl.BlockSpec(memory_space=pltpu.VMEM)
    given = [a for _, _, arrays in blocks for a in arrays] + ([] if acc is None else [acc])
    out = [jax.ShapeDtypeStruct((HALF, VECS), jnp.float32)] * 2 if last else [jax.ShapeDtypeStruct((LOCAL, VECS), jnp.float32)]
    scratch = [pltpu.VMEM((len(blocks), 2 * HALF, VECS), jnp.bfloat16)]
    if fetch:
        out = out + [jax.ShapeDtypeStruct(operator.shape, operator.dtype)]
        scratch = scratch + [pltpu.SemaphoreType.DMA((BLOCKS,))]
    return pl.pallas_call(
        functools.partial(product_kernel, tuple((t, z, len(arrays)) for t, z, arrays in blocks), fetch, acc is not None, last),
        in_specs=[pl.BlockSpec(memory_space=pl.ANY) if fetch else vmem] + [vmem] * len(given),
        out_specs=[vmem] * len(out),
        out_shape=out,
        scratch_shapes=scratch,
        compiler_params=pltpu.CompilerParams(vmem_limit_bytes=20 << 20),
    )(operator, *given)


def on_device(coupling, vectors):
    core = lax.axis_index("core")
    operator = split_operator(coupling)

    def along_first(rows):
        near = {s: send(rows, FIRST[s]) for s in (2, 1, 3)}
        return jnp.concatenate([rows, near[1], near[2], near[3]], axis=0)

    def beside(rows):
        return send(rows, SECOND[1]), send(rows, SECOND[3])

    def opposite(low, high):
        return send(low[: 2 * SH], SECOND[1]), send(high[2 * SH :], SECOND[3])

    def apply(current):
        partner = send(current, SWAP_ZH)
        a = along_first(current)
        b = along_first(partner)
        a1, a3 = beside(a)
        b1, b3 = beside(b)
        acc, fast = product(operator, [(0, 0, [a]), (0, 1, [b])], None, fetch=True)
        acc, a1, a3 = lax.optimization_barrier((acc, a1, a3))
        a2 = opposite(a1, a3)
        (acc,) = product(fast, [(1, 0, [a1]), (3, 0, [a3])], acc)
        acc, b1, b3 = lax.optimization_barrier((acc, b1, b3))
        b2 = opposite(b1, b3)
        (acc,) = product(fast, [(1, 1, [b1]), (3, 1, [b3]), (2, 0, a2)], acc)
        keep, give = product(fast, [(2, 1, b2)], acc, last=True)
        total = keep + send(give, SWAP_CORE)
        here = {s: send(total[s * SH : (s + 1) * SH], ALONG_ZL[s]) for s in (2, 1, 3)}
        return (total[:SH] + here[1]) + (here[2] + here[3])

    def step(_, carry):
        _, previous, current = carry
        applied = apply(current)
        following = (2.0 / filter_half) * (applied - filter_center * current) - previous
        return previous, current, following

    at_lower = (filter_lower - filter_center) / filter_half
    before, scale = 1.0, at_lower
    for _ in range(DEGREE - 1):
        before, scale = scale, 2.0 * at_lower * scale - before
    zero = jnp.zeros_like(vectors)
    older, _, current = lax.fori_loop(0, DEGREE, step, (zero, zero, vectors))
    current = (0.5 / scale) * (current - older)

    local = jnp.dot(current.T, current, precision=lax.Precision.HIGHEST, preferred_element_type=jnp.float32)
    halves = local.reshape(2, 128, VECS)
    mine = lax.dynamic_index_in_dim(halves, core, 0, keepdims=False)
    other = lax.dynamic_index_in_dim(halves, 1 - core, 0, keepdims=False)
    half = mine + send(other, SWAP_CORE)
    piece = lax.all_to_all(half.reshape(16, 8, VECS), ("x", "y"), 0, 0).sum(axis=0)
    every = lax.all_to_all(jnp.broadcast_to(piece, (8, 8, VECS)), ("zh", "zl"), 0, 0).sum(axis=0) / ORDER
    half = lax.all_to_all(jnp.broadcast_to(every, (16, 8, VECS)), ("x", "y"), 0, 0).reshape(128, VECS)
    other = send(half, SWAP_CORE)
    gram = jnp.concatenate([jnp.where(core == 0, half, other), jnp.where(core == 0, other, half)], axis=0)
    return current, gram


def solution(mesh):
    fine = Mesh(mesh.devices.reshape(DIMS), AX)
    return jax.shard_map(
        on_device,
        mesh=fine,
        in_specs=(P(("x", "zh", "y"), ("zl", "core")), P(AX, None)),
        out_specs=(P(AX, None), P()),
        check_vma=False,
    )
```

```python
import functools

import jax
import jax.numpy as jnp
from jax import lax
from jax.experimental import pallas as pl
from jax.experimental.pallas import tpu as pltpu
from jax.sharding import Mesh, PartitionSpec as P


ORDER = 24576
VECS = 256
DEGREE = 6
SH = 96
LOCAL = 768
COLS = 3072

filter_center = 2.75
filter_half = 1.75
filter_lower = 0.0


AX = ("x", "zh", "y", "zl", "core")
DIMS = (4, 2, 4, 4, 2)


def lin(x, zh, y, zl, core):
    return (((x * 2 + zh) * 4 + y) * 4 + zl) * 2 + core


def pairs(move):
    out = []
    for x in range(4):
        for zh in range(2):
            for y in range(4):
                for zl in range(4):
                    for core in range(2):
                        out.append((lin(x, zh, y, zl, core), lin(*move(x, zh, y, zl, core))))
    return out


SWAP_CORE = pairs(lambda x, zh, y, zl, core: (x, zh, y, zl, 1 - core))
SWAP_ZH = pairs(lambda x, zh, y, zl, core: (x, 1 - zh, y, zl, core))


def along_y(x, zh, y, zl, core, s):
    return (x, zh, (y + s) % 4, zl, core)


def along_x(x, zh, y, zl, core, s):
    return ((x + s) % 4, zh, y, zl, core)


FIRST = [pairs(lambda x, zh, y, zl, core, s=s: (along_x if core else along_y)(x, zh, y, zl, core, s)) for s in range(4)]
SECOND = [pairs(lambda x, zh, y, zl, core, s=s: (along_y if core else along_x)(x, zh, y, zl, core, s)) for s in range(4)]
ALONG_ZL = [pairs(lambda x, zh, y, zl, core, s=s: (x, zh, y, (zl + s) % 4, core)) for s in range(4)]


def send(value, moves):
    return lax.ppermute(value, AX, moves)


HALF = 4 * SH
BLOCKS = 4
WIDE = COLS // BLOCKS
LANES = 128


def position():
    x, zh, y, zl, core = (lax.axis_index(a) for a in AX)
    return core, zl, zh, jnp.where(core == 0, x, y), jnp.where(core == 0, y, x)


def split_kernel(h_ref, out_ref):
    core = position()[0]

    def write(order):
        h = h_ref[...]
        for block in range(BLOCKS):
            part = jnp.concatenate([h[:, i * SH : (i + 1) * SH] for i in order[8 * block : 8 * block + 8]], axis=1)
            hi = part.astype(jnp.bfloat16)
            out_ref[block, :, :WIDE] = hi
            out_ref[block, :, WIDE:] = (part - hi.astype(jnp.float32)).astype(jnp.bfloat16)

    @pl.when(core == 0)
    def _():
        write(list(range(32)))

    @pl.when(core != 0)
    def _():
        write([(x * 2 + zh) * 4 + y for y in range(4) for zh in range(2) for x in range(4)])


def split_operator(coupling):
    return pl.pallas_call(
        split_kernel,
        grid=(LOCAL // 96,),
        in_specs=[pl.BlockSpec((96, COLS), lambda i: (i, 0))],
        out_specs=pl.BlockSpec((BLOCKS, 96, 2 * WIDE), lambda i: (0, i, 0)),
        out_shape=jax.ShapeDtypeStruct((BLOCKS, LOCAL, 2 * WIDE), jnp.bfloat16),
        compiler_params=pltpu.CompilerParams(vmem_limit_bytes=16 << 20),
    )(coupling)


def product_kernel(steps, has_acc, last, *refs):
    operator, refs = refs[0], refs[1:]
    parts, refs = refs[: len(steps)], refs[len(steps) :]
    acc_in, refs = (refs[0], refs[1:]) if has_acc else (None, refs)
    outs, rows_of = refs[:-1], refs[-1]
    core, zl, zh, own_u, own_v = position()
    for b, part in enumerate(parts):
        for s in range(4):
            for z in range(2):
                rows = part[(s * 2 + z) * SH : (s * 2 + z + 1) * SH, :]
                hi = rows.astype(jnp.bfloat16)
                lo = (rows - hi.astype(jnp.float32)).astype(jnp.bfloat16)
                at = pl.multiple_of(((zh + z) % 2) * HALF + ((own_v - s + 4) % 4) * SH, SH)
                rows_of[b, pl.ds(at, SH), :LANES] = hi
                rows_of[b, pl.ds(at, SH), LANES:] = lo
    for half in range(2):
        m = slice(half * LOCAL // 2, (half + 1) * LOCAL // 2)
        acc = acc_in[m, :] if has_acc else None
        for b, t in enumerate(steps):
            block = (own_u - t + 4) % 4
            both = jnp.dot(operator[block, m, :WIDE], rows_of[b], preferred_element_type=jnp.float32)
            term = jnp.dot(operator[block, m, WIDE:], rows_of[b, :, :LANES], preferred_element_type=jnp.float32)
            term += both[:, LANES:]
            term += both[:, :LANES]
            acc = term if acc is None else acc + term
        if not last:
            outs[0][m, :] = acc
            continue
        keep, give = outs
        for pair in range(2):
            to = pl.multiple_of(((half * 2 + pair - zl + 4) % 4) * SH, SH)
            even, odd = acc[pair * 2 * SH : pair * 2 * SH + SH], acc[pair * 2 * SH + SH : (pair + 1) * 2 * SH]

            @pl.when(core == 0)
            def _():
                keep[pl.ds(to, SH), :] = even
                give[pl.ds(to, SH), :] = odd

            @pl.when(core != 0)
            def _():
                keep[pl.ds(to, SH), :] = odd
                give[pl.ds(to, SH), :] = even


def product(operator, parts, acc, last=False):
    vmem = pl.BlockSpec(memory_space=pltpu.VMEM)
    args = [operator, *parts.values()] + ([] if acc is None else [acc])
    shape = [(HALF, LANES)] * 2 if last else [(LOCAL, LANES)]
    out = pl.pallas_call(
        functools.partial(product_kernel, tuple(parts), acc is not None, last),
        in_specs=[vmem] * len(args),
        out_specs=[vmem] * len(shape),
        out_shape=[jax.ShapeDtypeStruct(a, jnp.float32) for a in shape],
        scratch_shapes=[pltpu.VMEM((len(parts), WIDE, 2 * LANES), jnp.bfloat16)],
        compiler_params=pltpu.CompilerParams(vmem_limit_bytes=16 << 20),
    )(*args)
    return out if last else out[0]


def on_device(coupling, vectors):
    core = lax.axis_index("core")
    operator = split_operator(coupling)

    def gather(current):
        partner = send(current, SWAP_ZH)
        plane = jnp.concatenate([current, partner], axis=0)
        near = {s: send(plane, FIRST[s]) for s in (2, 1, 3)}
        first = jnp.concatenate([plane, near[1], near[2], near[3]], axis=0)
        return first, {s: send(first, SECOND[s]) for s in (2, 1, 3)}

    def apply(current):
        first, far = gather(current)
        acc = product(operator, {0: first}, None)
        acc = product(operator, {1: far[1], 3: far[3]}, acc)
        keep, give = product(operator, {2: far[2]}, acc, last=True)
        total = keep + send(give, SWAP_CORE)
        here = {s: send(total[s * SH : (s + 1) * SH], ALONG_ZL[s]) for s in (2, 1, 3)}
        return (total[:SH] + here[1]) + (here[2] + here[3])

    streams = lax.optimization_barrier((vectors[:, :LANES], vectors[:, LANES:]))
    states = [(v, v) for v in streams]
    sigma_first = filter_half / (filter_lower - filter_center)
    sigma_now = sigma_first
    for degree_index in range(DEGREE):
        sigma_new = 1.0 / (2.0 / sigma_first - sigma_now)
        gain, loss = 2.0 * sigma_new / filter_half, sigma_now * sigma_new
        if degree_index == 0:
            sigma_new, gain, loss = sigma_first, sigma_first / filter_half, None
        for i, (previous, current) in enumerate(states):
            following = gain * (apply(current) - filter_center * current)
            if loss is not None:
                following = following - loss * previous
            states[i] = (current, following)
        sigma_now = sigma_new
    current = jnp.concatenate([following for _, following in states], axis=1)

    local = jnp.dot(current.T, current, precision=lax.Precision.HIGHEST, preferred_element_type=jnp.float32)
    halves = local.reshape(2, 128, VECS)
    mine = lax.dynamic_index_in_dim(halves, core, 0, keepdims=False)
    other = lax.dynamic_index_in_dim(halves, 1 - core, 0, keepdims=False)
    half = mine + send(other, SWAP_CORE)
    piece = lax.all_to_all(half.reshape(16, 8, VECS), ("x", "y"), 0, 0).sum(axis=0)
    every = lax.all_to_all(jnp.broadcast_to(piece, (8, 8, VECS)), ("zh", "zl"), 0, 0).sum(axis=0) / ORDER
    half = lax.all_to_all(jnp.broadcast_to(every, (16, 8, VECS)), ("x", "y"), 0, 0).reshape(128, VECS)
    other = send(half, SWAP_CORE)
    gram = jnp.concatenate([jnp.where(core == 0, half, other), jnp.where(core == 0, other, half)], axis=0)
    return current, gram


def solution(mesh):
    fine = Mesh(mesh.devices.reshape(DIMS), AX)
    return jax.shard_map(
        on_device,
        mesh=fine,
        in_specs=(P(("x", "zh", "y"), ("zl", "core")), P(AX, None)),
        out_specs=(P(AX, None), P()),
        check_vma=False,
    )
```

```python
import functools

import jax
import jax.numpy as jnp
from jax import lax
from jax.experimental import pallas as pl
from jax.experimental.pallas import tpu as pltpu
from jax.sharding import Mesh, PartitionSpec as P

ORDER = 24576
VECS = 256
DEGREE = 6
SH = 96
LOCAL = 768
COLS = 3072

filter_center = 2.75
filter_half = 1.75
filter_lower = 0.0


AX = ("x", "zh", "y", "zl", "core")
DIMS = (4, 2, 4, 4, 2)


def lin(x, zh, y, zl, core):
    return (((x * 2 + zh) * 4 + y) * 4 + zl) * 2 + core


def pairs(move):
    out = []
    for x in range(4):
        for zh in range(2):
            for y in range(4):
                for zl in range(4):
                    for core in range(2):
                        out.append((lin(x, zh, y, zl, core), lin(*move(x, zh, y, zl, core))))
    return out


SWAP_CORE = pairs(lambda x, zh, y, zl, core: (x, zh, y, zl, 1 - core))
SWAP_ZH = pairs(lambda x, zh, y, zl, core: (x, 1 - zh, y, zl, core))


def along_y(x, zh, y, zl, core, s):
    return (x, zh, (y + s) % 4, zl, core)


def along_x(x, zh, y, zl, core, s):
    return ((x + s) % 4, zh, y, zl, core)


FIRST = [pairs(lambda x, zh, y, zl, core, s=s: (along_x if core else along_y)(x, zh, y, zl, core, s)) for s in range(4)]
SECOND = [pairs(lambda x, zh, y, zl, core, s=s: (along_y if core else along_x)(x, zh, y, zl, core, s)) for s in range(4)]
ALONG_ZL = [pairs(lambda x, zh, y, zl, core, s=s: (x, zh, y, (zl + s) % 4, core)) for s in range(4)]


def send(value, moves):
    return lax.ppermute(value, AX, moves)


HALF = 4 * SH
BLOCKS = COLS // HALF


def position():
    x, zh, y, zl, core = (lax.axis_index(a) for a in AX)
    return core, zl, zh, jnp.where(core == 0, x, y), jnp.where(core == 0, y, x)


def split_kernel(h_ref, out_ref):
    core = position()[0]

    def write(order):
        h = h_ref[...]
        for block in range(BLOCKS):
            part = jnp.concatenate([h[:, i * SH : (i + 1) * SH] for i in order[4 * block : 4 * block + 4]], axis=1)
            hi = part.astype(jnp.bfloat16)
            out_ref[block, :, :HALF] = hi
            out_ref[block, :, HALF:] = (part - hi.astype(jnp.float32)).astype(jnp.bfloat16)

    @pl.when(core == 0)
    def _():
        write(list(range(32)))

    @pl.when(core != 0)
    def _():
        write([(x * 2 + zh) * 4 + y for y in range(4) for zh in range(2) for x in range(4)])


def split_operator(coupling):
    return pl.pallas_call(
        split_kernel,
        grid=(LOCAL // 96,),
        in_specs=[pl.BlockSpec((96, COLS), lambda i: (i, 0))],
        out_specs=pl.BlockSpec((BLOCKS, 96, 2 * HALF), lambda i: (0, i, 0)),
        out_shape=jax.ShapeDtypeStruct((BLOCKS, LOCAL, 2 * HALF), jnp.bfloat16),
        compiler_params=pltpu.CompilerParams(vmem_limit_bytes=16 << 20),
    )(coupling)


def product_kernel(blocks, fetch, has_acc, last, *refs):
    operator, refs = refs[0], refs[1:]
    n = sum(count for _, _, count in blocks)
    parts, refs = refs[:n], refs[n:]
    acc_in, refs = (refs[0], refs[1:]) if has_acc else (None, refs)
    outs, refs = (refs[:2], refs[2:]) if last else (refs[:1], refs[1:])
    core, zl, zh, own_u, own_v = position()

    def block_of(t, z):
        return ((own_u - t + 4) % 4) * 2 + (zh + z) % 2

    copies = []
    if fetch:
        whole, refs = refs[0], refs[1:]
        sems = refs[1]
        for k in range(BLOCKS):
            block = block_of(k // 2, k % 2)
            copies.append(pltpu.make_async_copy(operator.at[block], whole.at[block], sems.at[k]))
            copies[-1].start()
        operator = whole
    rows_of = refs[0]

    pieces = iter(parts)
    for b, (_, _, count) in enumerate(blocks):
        for s in range(4):
            if s % (4 // count) == 0:
                part = next(pieces)
            first = s % (4 // count) * SH
            rows = part[first : first + SH, :]
            hi = rows.astype(jnp.bfloat16)
            lo = (rows - hi.astype(jnp.float32)).astype(jnp.bfloat16)
            at = pl.multiple_of(((own_v - s + 4) % 4) * SH, SH)
            rows_of[b, pl.ds(at, SH), :] = lo
            rows_of[b, pl.ds(HALF + at, SH), :] = hi
    for copy in copies[: len(blocks)]:
        copy.wait()
    for half in range(2):
        m = slice(half * LOCAL // 2, (half + 1) * LOCAL // 2)
        acc = acc_in[m, :] if has_acc else None
        for b, (t, z, _) in enumerate(blocks):
            block = block_of(t, z)
            term = jnp.dot(operator[block, m, :], rows_of[b], preferred_element_type=jnp.float32)
            term += jnp.dot(operator[block, m, :HALF], rows_of[b, HALF:, :], preferred_element_type=jnp.float32)
            acc = term if acc is None else acc + term
        if not last:
            outs[0][m, :] = acc
            continue
        keep, give = outs
        for pair in range(2):
            to = pl.multiple_of(((half * 2 + pair - zl + 4) % 4) * SH, SH)
            even, odd = acc[pair * 2 * SH : pair * 2 * SH + SH], acc[pair * 2 * SH + SH : (pair + 1) * 2 * SH]

            keep[pl.ds(to, SH), :] = jnp.where(core == 0, even, odd)
            give[pl.ds(to, SH), :] = jnp.where(core == 0, odd, even)

    for copy in copies[len(blocks) :]:
        copy.wait()


def product(operator, blocks, acc, fetch=False, last=False):
    vmem = pl.BlockSpec(memory_space=pltpu.VMEM)
    given = [a for _, _, arrays in blocks for a in arrays] + ([] if acc is None else [acc])
    out = [jax.ShapeDtypeStruct((HALF, VECS), jnp.float32)] * 2 if last else [jax.ShapeDtypeStruct((LOCAL, VECS), jnp.float32)]
    scratch = [pltpu.VMEM((len(blocks), 2 * HALF, VECS), jnp.bfloat16)]
    if fetch:
        out = out + [jax.ShapeDtypeStruct(operator.shape, operator.dtype)]
        scratch = scratch + [pltpu.SemaphoreType.DMA((BLOCKS,))]
    return pl.pallas_call(
        functools.partial(product_kernel, tuple((t, z, len(arrays)) for t, z, arrays in blocks), fetch, acc is not None, last),
        in_specs=[pl.BlockSpec(memory_space=pl.ANY) if fetch else vmem] + [vmem] * len(given),
        out_specs=[vmem] * len(out),
        out_shape=out,
        scratch_shapes=scratch,
        compiler_params=pltpu.CompilerParams(vmem_limit_bytes=20 << 20),
    )(operator, *given)


def on_device(coupling, vectors):
    core = lax.axis_index("core")
    operator = split_operator(coupling)

    def along_first(rows):
        near = {s: send(rows, FIRST[s]) for s in (2, 1, 3)}
        return jnp.concatenate([rows, near[1], near[2], near[3]], axis=0)

    def along_second(rows):
        return {s: send(rows, SECOND[s]) for s in (2, 1, 3)}

    def apply(current):
        partner = send(current, SWAP_ZH)
        a = along_first(current)
        far_a = along_second(a)
        b = along_first(partner)
        far_b = along_second(b)
        acc, fast = product(operator, [(0, 0, [a]), (0, 1, [b])], None, fetch=True)
        (acc,) = product(fast, [(t, 0, [far_a[t]]) for t in (1, 3, 2)], acc)
        (acc,) = product(fast, [(t, 1, [far_b[t]]) for t in (1, 3)], acc)
        keep, give = product(fast, [(2, 1, [far_b[2]])], acc, last=True)
        total = keep + send(give, SWAP_CORE)
        here = {s: send(total[s * SH : (s + 1) * SH], ALONG_ZL[s]) for s in (2, 1, 3)}
        return (total[:SH] + here[1]) + (here[2] + here[3])

    def step(_, carry):
        older, previous, current = carry
        following = (2.0 / filter_half) * (apply(current) - filter_center * current) - previous
        return previous, current, following

    at_lower = (filter_lower - filter_center) / filter_half
    before, scale = 1.0, at_lower
    for _ in range(DEGREE - 1):
        before, scale = scale, 2.0 * at_lower * scale - before
    zero = jnp.zeros_like(vectors)
    older, _, current = lax.fori_loop(1, DEGREE, step, step(0, (zero, zero, vectors)))
    current = (0.5 / scale) * (current - older)

    local = jnp.dot(current.T, current, precision=lax.Precision.HIGHEST, preferred_element_type=jnp.float32)
    halves = local.reshape(2, 128, VECS)
    mine = lax.dynamic_index_in_dim(halves, core, 0, keepdims=False)
    other = lax.dynamic_index_in_dim(halves, 1 - core, 0, keepdims=False)
    half = mine + send(other, SWAP_CORE)
    piece = lax.all_to_all(half.reshape(16, 8, VECS), ("x", "y"), 0, 0).sum(axis=0)
    every = lax.all_to_all(jnp.broadcast_to(piece, (8, 8, VECS)), ("zh", "zl"), 0, 0).sum(axis=0) / ORDER
    half = lax.all_to_all(jnp.broadcast_to(every, (16, 8, VECS)), ("x", "y"), 0, 0).reshape(128, VECS)
    other = send(half, SWAP_CORE)
    gram = jnp.concatenate([jnp.where(core == 0, half, other), jnp.where(core == 0, other, half)], axis=0)
    return current, gram


def solution(mesh):
    fine = Mesh(mesh.devices.reshape(DIMS), AX)
    return jax.shard_map(
        on_device,
        mesh=fine,
        in_specs=(P(("x", "zh", "y"), ("zl", "core")), P(AX, None)),
        out_specs=(P(AX, None), P()),
        check_vma=False,
    )
```
